32 devices in a mesh: groups: 1, px: 16 (over z, y, x), py: 2 (over core).
Axes of the slice: x: 2, y: 2, z: 4, core: 2. Of those that a mesh axis runs over, the one named last changes fastest.
Arguments:
- field: bfloat16 [1, 20, 384, 192, 128], P('groups', None, 'px', 'py'), may hold values from -6 to 6
- spectral_weight: bfloat16 [2, 20, 20, 1536, 96], P(None, None, None, ('py', 'px')), may hold values from -6 to 6
- pointwise_weight: bfloat16 [20, 20], replicated, may hold values from -1.25 to 1.25
- bias: float32 [20], replicated, may hold values from -3 to 3
Outputs:
- mixed_field: bfloat16 [1, 20, 384, 192, 128], P('groups', None, 'px', 'py')
The draws below stay inside these ranges and needn't reach their ends.
All inputs are finite; a program needn't handle non-finite values.
Results may differ from the reference program's by a relative error of at most 0.001.
Values sent between devices are 32-bit elements; how exact they have to be, the bound alone decides.
A program may use at most 192 MiB of HBM per device.

```python
import jax
import jax.numpy as jnp
from jax import lax

B = 1
C = 20
NX = 384
NY = 192
NZ = 128
MX = 96
MY = 48
MZ = 32


def block_scale(rng, shape, split, smallest, largest):
    loudness, own = 1.0, jax.random.fold_in(rng, 6)
    for axis_at, shards_of in split:
        steps = jnp.exp(jax.random.uniform(jax.random.fold_in(own, axis_at), (shards_of,), jnp.float32, smallest / len(split), largest / len(split)))
        loudness = loudness * jnp.repeat(steps, shape[axis_at] // shards_of).reshape([-1 if axis == axis_at else 1 for axis in range(len(shape))])
    return loudness


def centred(key, shape, deviation, bound, shards=(), kind=jnp.bfloat16):
    result = jax.random.normal(key, shape, jnp.float32) * deviation
    if len(shards) > 0:
        result = block_scale(key, shape, shards, -0.22, 0.18) * result
    return jnp.clip(result, min=-bound, max=bound).astype(kind)


def setup_inputs(seed: int = 0, part: int = 0) -> dict:
    arg_keys = jax.random.split(jax.random.key(seed), 5)
    part_keys = jax.random.split(jax.random.fold_in(arg_keys[4], part), 5)
    field = centred(part_keys[0], (B, C, NX, NY, NZ), 1.0, 6.0, ((2, 16), (3, 2)))
    spectral_weight = centred(arg_keys[1], (2, C, C, MZ * MY, MX), 0.9, 6.0, ((3, 32),))
    pointwise_weight = centred(arg_keys[2], (C, C), C ** -0.5, 1.25)
    bias = centred(arg_keys[3], (C,), 0.5, 3.0, (), jnp.float32)
    return dict(field=field, spectral_weight=spectral_weight, pointwise_weight=pointwise_weight, bias=bias)


def spread_axis(values, axis, length):
    kept = values.shape[axis]
    half = kept // 2
    lower = lax.slice_in_dim(values, 0, half, axis=axis)
    upper = lax.slice_in_dim(values, half, kept, axis=axis)
    shape = list(values.shape)
    shape[axis] = length - kept
    return jnp.concatenate([lower, jnp.zeros(shape, values.dtype), upper], axis)


def mix_modes(weight_part, values):
    return jnp.einsum("iozyx,izyx->ozyx", weight_part, values, precision=lax.Precision.HIGHEST)


def reference(field, spectral_weight, pointwise_weight, bias):
    weights = spectral_weight.astype(jnp.float32).reshape(2, C, C, MZ, MY, MX)
    results = []
    for sample in range(B):
        volume = field[sample]

        def forward(channel):
            spectrum = jnp.fft.rfftn(channel.astype(jnp.float32))
            spectrum = jnp.concatenate([spectrum[:MX // 2], spectrum[NX - MX // 2:]], 0)
            spectrum = jnp.concatenate([spectrum[:, :MY // 2], spectrum[:, NY - MY // 2:]], 1)
            spectrum = jnp.transpose(spectrum[:, :, :MZ], (2, 1, 0))
            return jnp.real(spectrum), jnp.imag(spectrum)

        real_in, imag_in = lax.map(forward, volume)
        real_out = mix_modes(weights[0], real_in) - mix_modes(weights[1], imag_in)
        imag_out = mix_modes(weights[0], imag_in) + mix_modes(weights[1], real_in)
        flat_volume = volume.reshape(C, -1)

        def inverse(inputs):
            channel_index, real_part, imag_part = inputs
            parts = []
            for values in (real_part, imag_part):
                values = jnp.transpose(values, (2, 1, 0))
                values = spread_axis(values, 0, NX)
                values = spread_axis(values, 1, NY)
                values = jnp.pad(values, ((0, 0), (0, 0), (0, NZ // 2 + 1 - MZ)))
                parts.append(values)
            spectral = jnp.fft.irfftn(lax.complex(parts[0], parts[1]), s=(NX, NY, NZ))
            column = lax.dynamic_slice_in_dim(pointwise_weight, channel_index, 1, 1).reshape(1, C)
            local_part = jnp.dot(column, flat_volume, preferred_element_type=jnp.float32).reshape(NX, NY, NZ)
            total = spectral + local_part + lax.dynamic_slice_in_dim(bias, channel_index, 1, 0)[0]
            return jax.nn.gelu(total).astype(jnp.bfloat16)

        results.append(lax.map(inverse, (jnp.arange(C, dtype=jnp.int32), real_out, imag_out)))
    return jnp.stack(results)
```

```python
import functools

import jax
import jax.numpy as jnp
import numpy as np
from jax import lax
from jax.experimental import pallas as pl
from jax.experimental.pallas import tpu as pltpu
from jax.sharding import PartitionSpec as P

BF16 = jnp.bfloat16
F32 = jnp.float32


def kept(length, retained):
    index = np.arange(retained)
    return np.where(index < retained // 2, index, length - retained + index)


def angles(frequency, positions, length):
    return 2 * np.pi * (np.outer(frequency, positions) % length) / length


def split_np(table):
    high = table.astype(np.float32).astype(BF16)
    low = (table - high.astype(np.float64)).astype(np.float32).astype(BF16)
    return high, low


def split(values):
    high = values.astype(BF16)
    return high, (values - high.astype(F32)).astype(BF16)


def dot(a, b):
    return jnp.dot(a, b, preferred_element_type=F32)


def dot_nt(a, b):
    return lax.dot_general(a, b, (((1,), (1,)), ((), ())), preferred_element_type=F32)


def dot_tn(a, b):
    return lax.dot_general(a, b, (((0,), (0,)), ((), ())), preferred_element_type=F32)


def forward_kernel(direct, my, field_ref, t_ref, z_ref, own_ref, other_ref, g_high, g_low):
    channels, _, _, nz = field_ref.shape
    used, held = channels * my, g_high.shape[0]
    step = pl.program_id(0) * pl.num_programs(1) + pl.program_id(1)

    if held > used:
        @pl.when(step == 0)
        def _():
            g_high[used:] = jnp.zeros((held - used, 2 * nz), BF16)
            g_low[used:] = jnp.zeros((held - used, 2 * nz), BF16)

    table = t_ref[...]
    for c in range(channels):
        cells = field_ref[c, 0]
        high, low = split(dot(table, jnp.concatenate([cells, cells], 0)))
        rows = slice(c * my, (c + 1) * my)
        for q in range(2):
            g_high[rows, q * nz:(q + 1) * nz] = high[q * my:(q + 1) * my]
            g_low[rows, q * nz:(q + 1) * nz] = low[q * my:(q + 1) * my]
    modes = z_ref.shape[0] // 2
    first = dot_nt(z_ref[...], g_high[...])
    out = first[:modes] + first[modes:] + dot_nt(z_ref[:modes], g_low[...])
    half = modes // 2
    for ref, part in ((own_ref, out[:half]), (other_ref, out[half:])):
        if direct:
            tiles, xb = ref.shape[1:3]
            flat = ref.reshape(half * tiles * xb, 128)
            for t in range(tiles):
                flat[pl.ds(t * xb + pl.program_id(1), half, stride=tiles * xb), :] = part[
                    :, t * 128:(t + 1) * 128]
        else:
            ref[0] = part


def mix_kernel(got_ref, forward_high, forward_low, back_high, back_low, w_ref, out_ref,
               s_real, s_imag, m_high, m_low):
    o = pl.program_id(0)
    blocks, _, tiles, rows, _ = got_ref.shape
    channels, held, mx = s_real.shape
    modes = w_ref.shape[3]

    @pl.when(o == 0)
    def _():
        got = jnp.concatenate(
            [jnp.concatenate([got_ref[:, s, t].reshape(blocks * rows, 128) for t in range(tiles)], 1)
             for s in range(2)], 0)
        high, low = split(got)
        spectrum = dot_tn(high, forward_high[...]) + (
            dot_tn(low, forward_high[...]) + dot_tn(high, forward_low[...]))
        for i in range(channels):
            s_real[i] = spectrum[i * held:(i + 1) * held, :mx]
            s_imag[i] = spectrum[i * held:(i + 1) * held, 128:128 + mx]
        m_high[...] = jnp.zeros_like(m_high)
        m_low[...] = jnp.zeros_like(m_low)

    real = jnp.zeros((modes, mx), F32)
    imag = jnp.zeros((modes, mx), F32)
    for i in range(channels):
        w_real = w_ref[0, i, 0].astype(F32)
        w_imag = w_ref[1, i, 0].astype(F32)
        in_real = s_real[i, :modes]
        in_imag = s_imag[i, :modes]
        real += w_real * in_real - w_imag * in_imag
        imag += w_real * in_imag + w_imag * in_real
    at_row = pl.ds(pl.multiple_of(o * held, held), modes)
    for at, values in ((0, real), (128, imag)):
        high, low = split(values)
        m_high[at_row, at:at + mx] = high
        m_low[at_row, at:at + mx] = low

    @pl.when(o == pl.num_programs(0) - 1)
    def _():
        high = m_high[...]
        low = m_low[...]
        back = dot_nt(back_high[...], high) + (
            dot_nt(back_high[...], low) + dot_nt(back_low[...], high))
        for s in range(2):
            for t in range(tiles):
                out_ref[:, s, t] = back[
                    s * blocks * rows:(s + 1) * blocks * rows, t * 128:(t + 1) * 128
                ].reshape(blocks, rows, 128)


def inverse_kernel(direct, my, own_ref, other_ref, field_ref, z_ref, t_ref, pw_ref, bias_ref,
                   out_ref, v_high, v_low, local):
    channels, _, ny, nz = field_ref.shape
    group = 16
    for g in range(0, ny, 2 * group):
        pair = [field_ref[:, 0, g + k * group:g + (k + 1) * group, :].reshape(channels * group, nz)
                for k in range(2)]
        both = dot(pw_ref[...], jnp.concatenate(pair, 1))
        for k in range(2):
            local[:, g + k * group:g + (k + 1) * group, :] = both[:, k * nz:(k + 1) * nz].reshape(
                channels, group, nz)
    parts = []
    for ref in (own_ref, other_ref):
        if direct:
            half, tiles, xb, _ = ref.shape
            flat = ref.reshape(half * tiles * xb, 128)
            parts.append(jnp.concatenate(
                [flat[pl.ds(t * xb + pl.program_id(1), half, stride=tiles * xb), :]
                 for t in range(tiles)], 1))
        else:
            parts.append(ref[0])
    high, low = split(jnp.concatenate(parts, 0))
    v = dot_tn(jnp.concatenate([high, low, high], 0), z_ref[...])
    high, low = split(v)
    v_high[...] = high
    v_low[...] = low
    taps = 2 * my
    for c in range(channels):
        rows = slice(c * my, (c + 1) * my)
        top = [v_high[rows, q * nz:(q + 1) * nz] for q in range(2)]
        rest = [v_low[rows, q * nz:(q + 1) * nz] for q in range(2)]
        total = dot(t_ref[:, :2 * taps], jnp.concatenate(top + top, 0)) + dot(
            t_ref[:, :taps], jnp.concatenate(rest, 0))
        total = total + local[c] + bias_ref[c]
        out_ref[c, 0] = jax.nn.gelu(total).astype(BF16)


def whole_spec(shape):
    return pl.BlockSpec(shape, lambda *_: (0,) * len(shape))


def per_device(sizes, field, spectral_weight, pointwise_weight, bias):
    mx, my, mz = sizes
    samples, channels, x_local, y_local, nz = field.shape
    npx, npy = lax.axis_size("px"), lax.axis_size("py")
    assert samples == 1 and npy == 2
    nx, ny = x_local * npx, y_local * npy
    py = lax.axis_index("py")
    modes = spectral_weight.shape[3]
    per_kz = my // modes
    lanes_all = -(-channels * my // 128) * 128
    held = -(-modes // 16) * 16
    half = mz // npy * 2
    tiles = -(-channels * held // 128)
    direct = x_local % 8 == 0 and per_kz == 1
    halves = np.array([[0, 1], [1, 0]])

    y_angle = angles(kept(ny, my), np.arange(ny), ny)
    t_forward, t_back, z_forward, z_back = [], [], [], []
    z_angle = angles(np.arange(mz), np.arange(nz), nz)
    cosine, sine = np.cos(z_angle), np.sin(z_angle)
    weighting = (np.where(np.arange(mz) == 0, 1.0, 2.0) / (nx * ny * nz))[:, None, None]
    z_rows = np.stack([np.concatenate([cosine, -sine], 1), np.concatenate([-sine, -cosine], 1)], 1)
    z_inv = np.stack([np.concatenate([cosine, sine], 1), np.concatenate([-sine, cosine], 1)], 1) * weighting
    for p in range(npy):
        own = y_angle[:, p * y_local:(p + 1) * y_local]
        high, low = split_np(np.concatenate([np.cos(own), np.sin(own)], 0))
        t_forward.append(np.concatenate([high, low], 1))
        high, low = split_np(np.concatenate([np.cos(own), -np.sin(own)], 0).T)
        t_back.append(np.concatenate([high, low], 1))
        order = halves[p]
        rows = z_rows.reshape(npy, half, 2 * nz)[order].reshape(2 * half, 2 * nz)
        z_forward.append(np.concatenate(split_np(rows), 0))
        rows = z_inv.reshape(npy, half, 2 * nz)[order].reshape(2 * half, 2 * nz)
        high, low = split_np(rows)
        z_back.append(np.concatenate([high, high, low], 0))
    t_forward, t_back, z_forward, z_back = [
        lax.dynamic_index_in_dim(jnp.asarray(np.stack(table)), py, 0, keepdims=False)
        for table in (t_forward, t_back, z_forward, z_back)]

    x_angle = angles(kept(nx, mx), np.arange(nx), nx).T
    cosine, sine = np.cos(x_angle), np.sin(x_angle)
    x_forward = np.zeros((2, nx, 256))
    x_forward[0, :, :mx], x_forward[0, :, 128:128 + mx] = cosine, -sine
    x_forward[1, :, :mx], x_forward[1, :, 128:128 + mx] = sine, cosine
    x_back = np.zeros((2, nx, 256))
    x_back[0, :, :mx], x_back[0, :, 128:128 + mx] = cosine, -sine
    x_back[1, :, :mx], x_back[1, :, 128:128 + mx] = sine, cosine
    x_forward = [jnp.asarray(t.reshape(2 * nx, 256)) for t in split_np(x_forward)]
    x_back = [jnp.asarray(t.reshape(2 * nx, 256)) for t in split_np(x_back)]

    cells = field[0]
    xb = 8 if direct else 1
    grid = (x_local // xb, xb)
    field_spec = pl.BlockSpec((channels, 1, y_local, nz), lambda a, b: (0, a * xb + b, 0, 0))
    if direct:
        wide_shape = (half, tiles, x_local, 128)
        wide_spec = pl.BlockSpec((half, tiles, xb, 128), lambda a, b: (0, 0, a, 0))
    else:
        wide_shape = (x_local, half, lanes_all)
        wide_spec = pl.BlockSpec((1, half, lanes_all), lambda a, b: (a, 0, 0))
    limit = 60 * 2**20
    params = pltpu.CompilerParams(
        dimension_semantics=("arbitrary", "arbitrary"), vmem_limit_bytes=limit)
    own, other = pl.pallas_call(
        functools.partial(forward_kernel, direct, my),
        name="forward_yz",
        out_shape=[jax.ShapeDtypeStruct(wide_shape, F32)] * 2,
        grid=grid,
        in_specs=[field_spec, whole_spec(t_forward.shape), whole_spec(z_forward.shape)],
        out_specs=[wide_spec, wide_spec],
        scratch_shapes=[pltpu.VMEM((lanes_all, 2 * nz), BF16)] * 2,
        compiler_params=params,
    )(cells, t_forward, z_forward)

    swap = [(0, 1), (1, 0)]
    summed = own + lax.ppermute(other, "py", swap)
    if direct:
        got = lax.all_to_all(
            summed.reshape(npx, 2, tiles, x_local, 128), "px", split_axis=0, concat_axis=0, tiled=True)
    else:
        send = summed[:, :, :channels * my].reshape(
            x_local, half // 2, 2, channels, per_kz, modes).transpose(1, 4, 2, 0, 3, 5)
        got = lax.all_to_all(
            send.reshape(npx, 2, x_local, channels * modes), "px", split_axis=0, concat_axis=0,
            tiled=True)
        got = got.transpose(1, 0, 2, 3).reshape(2, nx, channels, modes)
        got = jnp.pad(got, ((0, 0), (0, 0), (0, 0), (0, held - modes)))
        got = jnp.pad(
            got.reshape(2, nx, channels * held),
            ((0, 0), (0, 0), (0, tiles * 128 - channels * held)))
        got = got.reshape(1, 2, nx, tiles, 128).transpose(0, 1, 3, 2, 4)
    mixed = pl.pallas_call(
        mix_kernel,
        name="mix_x",
        out_shape=jax.ShapeDtypeStruct(got.shape, F32),
        grid=(channels,),
        in_specs=[whole_spec(got.shape)] + [whole_spec((2 * nx, 256))] * 4 + [
            pl.BlockSpec((2, channels, 1, modes, mx), lambda o: (0, 0, o, 0, 0))],
        out_specs=whole_spec(got.shape),
        scratch_shapes=[pltpu.VMEM((channels, held, mx), F32)] * 2
        + [pltpu.VMEM((tiles * 128, 256), BF16)] * 2,
        compiler_params=pltpu.CompilerParams(
            dimension_semantics=("arbitrary",), vmem_limit_bytes=limit),
    )(got, *x_forward, *x_back, spectral_weight)
    if direct:
        back = lax.all_to_all(mixed, "px", split_axis=0, concat_axis=0, tiled=True)
        back = back.reshape(half, tiles, x_local, 128)
    else:
        mixed = mixed.transpose(0, 1, 3, 2, 4).reshape(2, npx, x_local, tiles * 128)
        mixed = mixed[..., :channels * held].reshape(2, npx, x_local, channels, held)[..., :modes]
        back = lax.all_to_all(
            mixed.transpose(1, 0, 2, 3, 4), "px", split_axis=0, concat_axis=0, tiled=True)
        back = back.reshape(half // 2, per_kz, 2, x_local, channels, modes).transpose(
            3, 0, 2, 4, 1, 5).reshape(x_local, half, channels * my)
        back = jnp.pad(back, ((0, 0), (0, 0), (0, lanes_all - channels * my)))
    partner = lax.ppermute(back, "py", swap)
    kron = jnp.kron(pointwise_weight.T.astype(F32), jnp.eye(16, dtype=F32)).astype(BF16)
    out = pl.pallas_call(
        functools.partial(inverse_kernel, direct, my),
        name="inverse_zy",
        out_shape=jax.ShapeDtypeStruct(cells.shape, BF16),
        grid=grid,
        in_specs=[wide_spec, wide_spec, field_spec, whole_spec(z_back.shape),
                  whole_spec(t_back.shape), whole_spec(kron.shape),
                  pl.BlockSpec(memory_space=pltpu.SMEM)],
        out_specs=field_spec,
        scratch_shapes=[pltpu.VMEM((lanes_all, 2 * nz), BF16)] * 2
        + [pltpu.VMEM((channels, y_local, nz), F32)],
        compiler_params=params,
    )(back, partner, cells, z_back, t_back, kron, bias)
    return out[None]


def solution(mesh):
    def per_part(field, spectral_weight, pointwise_weight, bias):
        rows, mx = spectral_weight.shape[3] * mesh.shape["px"] * mesh.shape["py"], spectral_weight.shape[4]
        mz = field.shape[4] // 4
        return per_device((mx, rows // mz, mz), field, spectral_weight, pointwise_weight, bias)

    in_specs = (
        P("groups", None, "px", "py", None),
        P(None, None, None, ("py", "px"), None),
        P(),
        P(),
    )
    out_specs = P("groups", None, "px", "py", None)
    return jax.shard_map(
        per_part, mesh=mesh, in_specs=in_specs, out_specs=out_specs, check_vma=False
    )
```

```python
import functools

import jax
import jax.numpy as jnp
import numpy as np
from jax import lax
from jax.experimental import pallas as pl
from jax.experimental.pallas import tpu as pltpu
from jax.sharding import PartitionSpec as P


BF16 = jnp.bfloat16
F32 = jnp.float32


def kept(length, retained):
    index = np.arange(retained)
    return np.where(index < retained // 2, index, length - retained + index)


def angles(frequency, positions, length):
    return 2 * np.pi * (np.outer(frequency, positions) % length) / length


def split_np(table):
    high = table.astype(np.float32).astype(BF16)
    low = (table - high.astype(np.float64)).astype(np.float32).astype(BF16)
    return high, low


def split(values):
    high = values.astype(BF16)
    return high, (values - high.astype(F32)).astype(BF16)


def dot(a, b):
    return jnp.dot(a, b, preferred_element_type=F32)


def dot_nt(a, b):
    return lax.dot_general(a, b, (((1,), (1,)), ((), ())), preferred_element_type=F32)


def dot_tn(a, b):
    return lax.dot_general(a, b, (((0,), (0,)), ((), ())), preferred_element_type=F32)


def forward_kernel(direct, my, units, *refs):
    fields, (t_ref, z_ref, own_ref, other_ref, g_high, g_low) = refs[:units], refs[units:]
    per_unit, _, _, nz = fields[0].shape
    table = t_ref[...]
    for c in range(units * per_unit):
        cells = fields[c // per_unit][c % per_unit, 0]
        high, low = split(dot(table, jnp.concatenate([cells, cells], 0)))
        rows = slice(c * my, (c + 1) * my)
        for q in range(2):
            g_high[rows, q * nz:(q + 1) * nz] = high[q * my:(q + 1) * my]
            g_low[rows, q * nz:(q + 1) * nz] = low[q * my:(q + 1) * my]
    modes = z_ref.shape[0] // 2
    first = dot_nt(z_ref[...], g_high[...])
    out = first[:modes] + first[modes:] + dot_nt(z_ref[:modes], g_low[...])
    out = jnp.concatenate([out[:modes // 2], out[modes // 2:]], 1)
    half = modes // 4
    for ref, part in ((own_ref, out[:half]), (other_ref, out[half:])):
        if direct:
            tiles, xb = ref.shape[1:3]
            flat = ref.reshape(half * tiles * xb, 128)
            for t in range(tiles):
                flat[pl.ds(t * xb + pl.program_id(1), half, stride=tiles * xb), :] = part[
                    :, t * 128:(t + 1) * 128]
        else:
            ref[0] = part


def mix_kernel(units, has_before, last, *refs):
    got_ref, forward_high, forward_low = refs[:3]
    weights, refs = refs[3:3 + units], refs[3 + units:]
    if has_before:
        before_ref, refs = refs[0], refs[1:]
    if last:
        back_high, back_low, out_ref, s_real, s_imag, m_high, m_low = refs
    else:
        out_ref, s_real, s_imag = refs
    o = pl.program_id(0)
    blocks, tiles, rows, _ = got_ref.shape
    channels, held, mx = s_real.shape
    per_unit = channels // units
    modes = weights[0].shape[3]
    lanes = channels * held

    @pl.when(o == 0)
    def _():
        got = jnp.concatenate(
            [got_ref[:, t].reshape(blocks * rows, 128) for t in range(tiles)], 1)
        high, low = split(jnp.concatenate([got[:, :lanes], got[:, lanes:2 * lanes]], 0))
        spectrum = dot_tn(high, forward_high[...]) + (
            dot_tn(low, forward_high[...]) + dot_tn(high, forward_low[...]))
        for i in range(channels):
            s_real[i] = spectrum[i * held:(i + 1) * held, :mx]
            s_imag[i] = spectrum[i * held:(i + 1) * held, 128:128 + mx]
        if last:
            m_high[...] = jnp.zeros_like(m_high)
            m_low[...] = jnp.zeros_like(m_low)

    if has_before:
        real, imag = before_ref[0, 0], before_ref[0, 1]
    else:
        real, imag = jnp.zeros((modes, mx), F32), jnp.zeros((modes, mx), F32)
    for i in range(channels):
        w_real = weights[i // per_unit][0, i % per_unit, 0].astype(F32)
        w_imag = weights[i // per_unit][1, i % per_unit, 0].astype(F32)
        in_real = s_real[i, :modes]
        in_imag = s_imag[i, :modes]
        real += w_real * in_real - w_imag * in_imag
        imag += w_real * in_imag + w_imag * in_real
    if not last:
        out_ref[0, 0] = real
        out_ref[0, 1] = imag
        return
    at_row = pl.ds(pl.multiple_of(o * held, held), modes)
    for at, values in ((0, real), (128, imag)):
        high, low = split(values)
        m_high[at_row, at:at + mx] = high
        m_low[at_row, at:at + mx] = low

    @pl.when(o == pl.num_programs(0) - 1)
    def _():
        high = m_high[...]
        low = m_low[...]
        back = dot_nt(back_high[...], high) + (
            dot_nt(back_high[...], low) + dot_nt(back_low[...], high))
        back = jnp.concatenate([back[:blocks * rows], back[blocks * rows:]], 1)
        for t in range(out_ref.shape[1]):
            out_ref[:, t] = back[:, t * 128:(t + 1) * 128].reshape(blocks, rows, 128)


def inverse_kernel(direct, my, start, chained, *refs):
    (own_ref, other_ref, field_ref, z_ref, t_ref, pw_ref, bias_ref) = refs[:7]
    out_ref, v_high, v_low, local = refs[7 + chained:]
    channels, _, ny, nz = field_ref.shape
    outs = out_ref.shape[0]
    group = 16
    for g in range(0, ny, 2 * group):
        pair = [field_ref[:, 0, g + k * group:g + (k + 1) * group, :].reshape(channels * group, nz)
                for k in range(2)]
        both = dot(pw_ref[...], jnp.concatenate(pair, 1))
        for k in range(2):
            local[:, g + k * group:g + (k + 1) * group, :] = both[:, k * nz:(k + 1) * nz].reshape(
                outs, group, nz)
    parts = []
    for ref in (own_ref, other_ref):
        if direct:
            half, tiles, xb, _ = ref.shape
            flat = ref.reshape(half * tiles * xb, 128)
            parts.append(jnp.concatenate(
                [flat[pl.ds(t * xb + pl.program_id(1), half, stride=tiles * xb), :]
                 for t in range(tiles)], 1))
        else:
            parts.append(ref[0])
    wide = jnp.concatenate(parts, 0)
    lanes = outs * my
    high, low = split(jnp.concatenate([wide[:, :lanes], wide[:, lanes:2 * lanes]], 0))
    high, low = split(dot_tn(jnp.concatenate([high, low, high], 0), z_ref[...]))
    v_high[...] = high
    v_low[...] = low
    taps = 2 * my
    for c in range(outs):
        rows = slice(c * my, (c + 1) * my)
        top = [v_high[rows, q * nz:(q + 1) * nz] for q in range(2)]
        rest = [v_low[rows, q * nz:(q + 1) * nz] for q in range(2)]
        total = dot(t_ref[:, :2 * taps], jnp.concatenate(top + top, 0)) + dot(
            t_ref[:, :taps], jnp.concatenate(rest, 0))
        total = total + local[c] + bias_ref[start + c]
        out_ref[c, 0] = jax.nn.gelu(total).astype(BF16)


def whole_spec(shape):
    return pl.BlockSpec(shape, lambda *_: (0,) * len(shape))


def per_device(sizes, field, spectral_weight, pointwise_weight, bias):
    mx, my, mz = sizes
    samples, channels, x_local, y_local, nz = field.shape
    npx, npy = lax.axis_size("px"), lax.axis_size("py")
    assert samples == 1 and npy == 2
    nx, ny = x_local * npx, y_local * npy
    py = lax.axis_index("py")
    modes = spectral_weight.shape[3]
    per_kz = my // modes
    held = -(-modes // 16) * 16
    half = mz // npy
    per_unit = 4 if channels % 4 == 0 else channels
    direct = x_local % 8 == 0 and per_kz == 1 and 2 * per_unit * my % 128 == 0
    every = list(range(channels // per_unit))
    halves = np.array([[0, 1], [1, 0]])

    y_angle = angles(kept(ny, my), np.arange(ny), ny)
    t_forward, t_back, z_forward, z_back = [], [], [], []
    z_angle = angles(np.arange(mz), np.arange(nz), nz)
    cosine, sine = np.cos(z_angle), np.sin(z_angle)
    weighting = (np.where(np.arange(mz) == 0, 1.0, 2.0) / (nx * ny * nz))[:, None]
    z_rows = np.stack([np.concatenate([cosine, -sine], 1), np.concatenate([-sine, -cosine], 1)], 0)
    z_inv = np.stack([np.concatenate([cosine, sine], 1), np.concatenate([-sine, cosine], 1)], 0) * weighting
    for p in range(npy):
        own = y_angle[:, p * y_local:(p + 1) * y_local]
        high, low = split_np(np.concatenate([np.cos(own), np.sin(own)], 0))
        t_forward.append(np.concatenate([high, low], 1))
        high, low = split_np(np.concatenate([np.cos(own), -np.sin(own)], 0).T)
        t_back.append(np.concatenate([high, low], 1))
        order = halves[p]
        rows = z_rows.reshape(2, npy, half, 2 * nz)[:, order].reshape(2 * mz, 2 * nz)
        z_forward.append(np.concatenate(split_np(rows), 0))
        rows = z_inv.reshape(2, npy, half, 2 * nz)[:, order].reshape(2 * mz, 2 * nz)
        high, low = split_np(rows)
        z_back.append(np.concatenate([high, high, low], 0))
    t_forward, t_back, z_forward, z_back = [
        lax.dynamic_index_in_dim(jnp.asarray(np.stack(table)), py, 0, keepdims=False)
        for table in (t_forward, t_back, z_forward, z_back)]

    x_angle = angles(kept(nx, mx), np.arange(nx), nx).T
    cosine, sine = np.cos(x_angle), np.sin(x_angle)
    x_forward = np.zeros((2, nx, 256))
    x_forward[0, :, :mx], x_forward[0, :, 128:128 + mx] = cosine, -sine
    x_forward[1, :, :mx], x_forward[1, :, 128:128 + mx] = sine, cosine
    x_back = np.zeros((2, nx, 256))
    x_back[0, :, :mx], x_back[0, :, 128:128 + mx] = cosine, -sine
    x_back[1, :, :mx], x_back[1, :, 128:128 + mx] = sine, cosine
    x_forward = [jnp.asarray(t.reshape(2 * nx, 256)) for t in split_np(x_forward)]
    x_back = [jnp.asarray(t.reshape(2 * nx, 256)) for t in split_np(x_back)]

    cells = field[0]
    xb = 8 if direct else 1
    grid = (x_local // xb, xb)
    limit = 60 * 2**20
    params = pltpu.CompilerParams(
        dimension_semantics=("arbitrary", "arbitrary"), vmem_limit_bytes=limit)
    swap = [(0, 1), (1, 0)]

    def field_spec(size, at):
        return pl.BlockSpec((size, 1, y_local, nz), lambda a, b: (at, a * xb + b, 0, 0))

    def wide_of(count):
        lanes = 2 * count * my
        if direct:
            return (half, lanes // 128, x_local, 128), pl.BlockSpec(
                (half, lanes // 128, xb, 128), lambda a, b: (0, 0, a, 0))
        return (x_local, half, lanes), pl.BlockSpec((1, half, lanes), lambda a, b: (a, 0, 0))

    def to_modes(units):
        count = len(units) * per_unit
        shape, spec = wide_of(count)
        own, other = pl.pallas_call(
            functools.partial(forward_kernel, direct, my, len(units)),
            name="forward_yz",
            out_shape=[jax.ShapeDtypeStruct(shape, F32)] * 2,
            grid=grid,
            in_specs=[field_spec(per_unit, u) for u in units]
            + [whole_spec(t_forward.shape), whole_spec(z_forward.shape)],
            out_specs=[spec, spec],
            scratch_shapes=[pltpu.VMEM((count * my, 2 * nz), BF16)] * 2,
            compiler_params=params,
            cost_estimate=pl.CostEstimate(
                flops=count * x_local * 40_000_000, transcendentals=0,
                bytes_accessed=count * x_local * y_local * nz * 4),
        )(*[cells] * len(units), t_forward, z_forward)
        summed = own + lax.ppermute(other, "py", swap)
        if direct:
            return lax.all_to_all(summed, "px", split_axis=0, concat_axis=0, tiled=True)
        send = summed.reshape(x_local, half, 2, count, per_kz, modes).transpose(1, 4, 2, 0, 3, 5)
        got = lax.all_to_all(
            send.reshape(npx, 2, x_local, count * modes), "px", split_axis=0, concat_axis=0,
            tiled=True)
        got = got.reshape(npx, 2, x_local, count, modes).transpose(0, 2, 1, 3, 4)
        got = jnp.pad(got, ((0, 0),) * 4 + ((0, held - modes),)).reshape(nx, 2 * count * held)
        tiles = -(-got.shape[1] // 128)
        got = jnp.pad(got, ((0, 0), (0, tiles * 128 - got.shape[1])))
        return got.reshape(1, nx, tiles, 128).transpose(0, 2, 1, 3)

    def mix(got, units, before, out_units):
        count, outs = len(units) * per_unit, len(out_units) * per_unit
        first = out_units[0] * per_unit
        last = before is not None or len(units) == len(every)
        blocks, _, rows, _ = got.shape

        def weight_spec(u):
            return pl.BlockSpec((2, per_unit, 1, modes, mx), lambda o: (0, u, first + o, 0, 0))

        specs = [whole_spec(got.shape)] + [whole_spec((2 * nx, 256))] * 2
        specs += [weight_spec(u) for u in units]
        operands = [got, *x_forward] + [spectral_weight] * len(units)
        if before is not None:
            specs.append(pl.BlockSpec((1, 2, modes, mx), lambda o: (first + o, 0, 0, 0)))
            operands.append(before)
        scratch = [pltpu.VMEM((count, held, mx), F32)] * 2
        if last:
            specs += [whole_spec((2 * nx, 256))] * 2
            operands += x_back
            shape = (blocks, -(-2 * outs * held // 128), rows, 128)
            out_spec = whole_spec(shape)
            padded = outs * held if direct else shape[1] * 64
            scratch += [pltpu.VMEM((padded, 256), BF16)] * 2
        else:
            shape = (outs, 2, modes, mx)
            out_spec = pl.BlockSpec((1, 2, modes, mx), lambda o: (o, 0, 0, 0))
        return pl.pallas_call(
            functools.partial(mix_kernel, len(units), before is not None, last),
            name="mix_x",
            out_shape=jax.ShapeDtypeStruct(shape, F32),
            grid=(outs,),
            in_specs=specs,
            out_specs=out_spec,
            scratch_shapes=scratch,
            compiler_params=pltpu.CompilerParams(
                dimension_semantics=("arbitrary",), vmem_limit_bytes=limit),
            cost_estimate=pl.CostEstimate(
                flops=count * outs * 40_000_000, transcendentals=0,
                bytes_accessed=4 * count * outs * modes * 128),
        )(*operands)

    def send_back(mixed, count):
        if direct:
            return lax.all_to_all(mixed, "px", split_axis=0, concat_axis=0, tiled=True)
        tiles = mixed.shape[1]
        mixed = mixed.transpose(0, 2, 1, 3).reshape(npx, x_local, tiles * 128)
        mixed = mixed[..., :2 * count * held].reshape(npx, x_local, 2, count, held)[..., :modes]
        back = lax.all_to_all(mixed, "px", split_axis=0, concat_axis=0, tiled=True)
        return back.reshape(half, per_kz, x_local, 2, count, modes).transpose(
            2, 0, 3, 4, 1, 5).reshape(x_local, half, 2 * count * my)

    kron = jnp.kron(pointwise_weight.T.astype(F32), jnp.eye(16, dtype=F32)).astype(BF16)

    def to_cells(back, units, so_far):
        count = len(units) * per_unit
        first = units[0] * per_unit
        partner = lax.ppermute(back, "py", swap)
        _, spec = wide_of(count)
        weights = kron[first * 16:(first + count) * 16]
        operands = [back, partner, cells, z_back, t_back, weights, bias]
        specs = [spec, spec, field_spec(channels, 0), whole_spec(z_back.shape),
                 whole_spec(t_back.shape), whole_spec(weights.shape),
                 pl.BlockSpec(memory_space=pltpu.SMEM)]
        chained = so_far is not None
        if chained:
            operands.append(so_far)
            specs.append(pl.BlockSpec(memory_space=pl.ANY))
        return pl.pallas_call(
            functools.partial(inverse_kernel, direct, my, first, int(chained)),
            name="inverse_zy",
            out_shape=jax.ShapeDtypeStruct(cells.shape, BF16),
            grid=grid,
            in_specs=specs,
            out_specs=field_spec(count, first // count),
            scratch_shapes=[pltpu.VMEM((count * my, 2 * nz), BF16)] * 2
            + [pltpu.VMEM((count, y_local, nz), F32)],
            input_output_aliases={7: 0} if chained else {},
            compiler_params=params,
            cost_estimate=pl.CostEstimate(
                flops=count * x_local * 60_000_000, transcendentals=0,
                bytes_accessed=count * x_local * y_local * nz * 6),
        )(*operands)

    if direct and len(every) == 5:
        in_chunks, out_chunks = [every[:2], every[2:]], [every[:2], every[2:4], every[4:]]
    else:
        in_chunks, out_chunks = [every], [every]
    before = None
    for units in in_chunks[:-1]:
        before = mix(to_modes(units), units, before, every)
    got = to_modes(in_chunks[-1])
    returned = []
    for units in out_chunks:
        mixed = mix(got, in_chunks[-1], before, units)
        returned.append(send_back(mixed, len(units) * per_unit))
    out = None
    for back, units in zip(returned, out_chunks):
        out = to_cells(back, units, out)
    return out[None]


def solution(mesh):
    def per_part(field, spectral_weight, pointwise_weight, bias):
        rows, mx = spectral_weight.shape[3] * mesh.shape["px"] * mesh.shape["py"], spectral_weight.shape[4]
        mz = field.shape[4] // 4
        return per_device((mx, rows // mz, mz), field, spectral_weight, pointwise_weight, bias)

    in_specs = (
        P("groups", None, "px", "py", None),
        P(None, None, None, ("py", "px"), None),
        P(),
        P(),
    )
    out_specs = P("groups", None, "px", "py", None)
    return jax.shard_map(
        per_part, mesh=mesh, in_specs=in_specs, out_specs=out_specs, check_vma=False
    )
```

```python
import functools

import jax
import jax.numpy as jnp
import numpy as np
from jax import lax
from jax.experimental import pallas as pl
from jax.experimental.pallas import tpu as pltpu
from jax.sharding import PartitionSpec as P


BF16 = jnp.bfloat16
F32 = jnp.float32


def kept(length, retained):
    index = np.arange(retained)
    return np.where(index < retained // 2, index, length - retained + index)


def angles(frequency, positions, length):
    return 2 * np.pi * (np.outer(frequency, positions) % length) / length


def split_np(table):
    high = table.astype(np.float32).astype(BF16)
    low = (table - high.astype(np.float64)).astype(np.float32).astype(BF16)
    return high, low


def split(values):
    high = values.astype(BF16)
    return high, (values - high.astype(F32)).astype(BF16)


def dot(a, b):
    return jnp.dot(a, b, preferred_element_type=F32)


def dot_nt(a, b):
    return lax.dot_general(a, b, (((1,), (1,)), ((), ())), preferred_element_type=F32)


def dot_tn(a, b):
    return lax.dot_general(a, b, (((0,), (0,)), ((), ())), preferred_element_type=F32)


def forward_kernel(direct, my, units, *refs):
    fields, (t_ref, z_ref, own_ref, other_ref), scratch = (
        refs[:units], refs[units:units + 4], refs[units + 4:])
    per_unit, count, _, nz = fields[0].shape
    table = t_ref[...]
    for k in range(count):
        g_high, g_low = scratch[2 * k:2 * k + 2]
        for c in range(units * per_unit):
            cells = fields[c // per_unit][c % per_unit, k]
            high, low = split(dot(table, jnp.concatenate([cells, cells], 0)))
            rows = slice(c * my, (c + 1) * my)
            for q in range(2):
                g_high[rows, q * nz:(q + 1) * nz] = high[q * my:(q + 1) * my]
                g_low[rows, q * nz:(q + 1) * nz] = low[q * my:(q + 1) * my]
    modes = z_ref.shape[0] // 2
    half = modes // 4
    for k in range(count):
        g_high, g_low = scratch[2 * k:2 * k + 2]
        first = dot_nt(z_ref[...], g_high[...])
        out = first[:modes] + first[modes:] + dot_nt(z_ref[:modes], g_low[...])
        out = jnp.concatenate([out[:modes // 2], out[modes // 2:]], 1)
        for ref, part in ((own_ref, out[:half]), (other_ref, out[half:])):
            if direct:
                tiles, xb = ref.shape[1:3]
                flat = ref.reshape(half * tiles * xb, 128)
                at = pl.program_id(1) * count + k
                for t in range(tiles):
                    flat[pl.ds(t * xb + at, half, stride=tiles * xb), :] = part[
                        :, t * 128:(t + 1) * 128]
            else:
                ref[0] = part


def mix_kernel(units, has_before, last, *refs):
    got_ref, forward_high, forward_low = refs[:3]
    weights, refs = refs[3:3 + units], refs[3 + units:]
    if has_before:
        before_ref, refs = refs[0], refs[1:]
    if last:
        back_high, back_low, out_ref, s_real, s_imag, m_high, m_low = refs
    else:
        out_ref, s_real, s_imag = refs
    o = pl.program_id(0)
    blocks, tiles, rows, _ = got_ref.shape
    channels, held, mx = s_real.shape
    per_unit = channels // units
    modes = weights[0].shape[3]
    lanes = channels * held

    @pl.when(o == 0)
    def _():
        got = jnp.concatenate(
            [got_ref[:, t].reshape(blocks * rows, 128) for t in range(tiles)], 1)
        high, low = split(jnp.concatenate([got[:, :lanes], got[:, lanes:2 * lanes]], 0))
        spectrum = dot_tn(high, forward_high[...]) + (
            dot_tn(low, forward_high[...]) + dot_tn(high, forward_low[...]))
        for i in range(channels):
            s_real[i] = spectrum[i * held:(i + 1) * held, :mx]
            s_imag[i] = spectrum[i * held:(i + 1) * held, 128:128 + mx]
        if last:
            m_high[...] = jnp.zeros_like(m_high)
            m_low[...] = jnp.zeros_like(m_low)

    if has_before:
        real, imag = before_ref[0, 0], before_ref[0, 1]
    else:
        real, imag = jnp.zeros((modes, mx), F32), jnp.zeros((modes, mx), F32)
    for i in range(channels):
        w_real = weights[i // per_unit][0, i % per_unit, 0].astype(F32)
        w_imag = weights[i // per_unit][1, i % per_unit, 0].astype(F32)
        in_real = s_real[i, :modes]
        in_imag = s_imag[i, :modes]
        real += w_real * in_real - w_imag * in_imag
        imag += w_real * in_imag + w_imag * in_real
    if not last:
        out_ref[0, 0] = real
        out_ref[0, 1] = imag
        return
    at_row = pl.ds(pl.multiple_of(o * held, held), modes)
    for at, values in ((0, real), (128, imag)):
        high, low = split(values)
        m_high[at_row, at:at + mx] = high
        m_low[at_row, at:at + mx] = low

    @pl.when(o == pl.num_programs(0) - 1)
    def _():
        high = m_high[...]
        low = m_low[...]
        back = dot_nt(back_high[...], high) + (
            dot_nt(back_high[...], low) + dot_nt(back_low[...], high))
        back = jnp.concatenate([back[:blocks * rows], back[blocks * rows:]], 1)
        for t in range(out_ref.shape[1]):
            out_ref[:, t] = back[:, t * 128:(t + 1) * 128].reshape(blocks, rows, 128)


def inverse_kernel(direct, my, start, chained, *refs):
    (own_ref, other_ref, field_ref, z_ref, t_ref, pw_ref, bias_ref) = refs[:7]
    out_ref, scratch = refs[7 + chained], refs[8 + chained:]
    channels, count, ny, nz = field_ref.shape
    outs = out_ref.shape[0]
    lanes = outs * my
    group = 16
    for k in range(count):
        v_high, v_low, local = scratch[3 * k:3 * k + 3]
        parts = []
        for ref in (own_ref, other_ref):
            if direct:
                half, tiles, xb, _ = ref.shape
                flat = ref.reshape(half * tiles * xb, 128)
                at = pl.program_id(1) * count + k
                parts.append(jnp.concatenate(
                    [flat[pl.ds(t * xb + at, half, stride=tiles * xb), :] for t in range(tiles)], 1))
            else:
                parts.append(ref[0])
        wide = jnp.concatenate(parts, 0)
        high, low = split(jnp.concatenate([wide[:, :lanes], wide[:, lanes:2 * lanes]], 0))
        high, low = split(dot_tn(jnp.concatenate([high, low, high], 0), z_ref[...]))
        v_high[...] = high
        v_low[...] = low
        for g in range(0, ny, 2 * group):
            pair = [field_ref[:, k, g + j * group:g + (j + 1) * group, :].reshape(
                channels * group, nz) for j in range(2)]
            both = dot(pw_ref[...], jnp.concatenate(pair, 1))
            for j in range(2):
                local[:, g + j * group:g + (j + 1) * group, :] = both[
                    :, j * nz:(j + 1) * nz].reshape(outs, group, nz)
    taps = 2 * my
    for k in range(count):
        v_high, v_low, local = scratch[3 * k:3 * k + 3]
        for c in range(outs):
            rows = slice(c * my, (c + 1) * my)
            top = [v_high[rows, q * nz:(q + 1) * nz] for q in range(2)]
            rest = [v_low[rows, q * nz:(q + 1) * nz] for q in range(2)]
            total = dot(t_ref[:, :2 * taps], jnp.concatenate(top + top, 0)) + dot(
                t_ref[:, :taps], jnp.concatenate(rest, 0))
            total = total + local[c] + bias_ref[start + c]
            out_ref[c, k] = jax.nn.gelu(total).astype(BF16)


def whole_spec(shape):
    return pl.BlockSpec(shape, lambda *_: (0,) * len(shape))


def per_device(sizes, field, spectral_weight, pointwise_weight, bias):
    mx, my, mz = sizes
    samples, channels, x_local, y_local, nz = field.shape
    npx, npy = lax.axis_size("px"), lax.axis_size("py")
    assert samples == 1 and npy == 2
    nx, ny = x_local * npx, y_local * npy
    py = lax.axis_index("py")
    modes = spectral_weight.shape[3]
    per_kz = my // modes
    held = -(-modes // 16) * 16
    half = mz // npy
    per_unit = 4 if channels % 4 == 0 else channels
    direct = x_local % 8 == 0 and per_kz == 1 and 2 * per_unit * my % 128 == 0
    every = list(range(channels // per_unit))
    halves = np.array([[0, 1], [1, 0]])

    y_angle = angles(kept(ny, my), np.arange(ny), ny)
    t_forward, t_back, z_forward, z_back = [], [], [], []
    z_angle = angles(np.arange(mz), np.arange(nz), nz)
    cosine, sine = np.cos(z_angle), np.sin(z_angle)
    weighting = (np.where(np.arange(mz) == 0, 1.0, 2.0) / (nx * ny * nz))[:, None]
    z_rows = np.stack([np.concatenate([cosine, -sine], 1), np.concatenate([-sine, -cosine], 1)], 0)
    z_inv = np.stack([np.concatenate([cosine, sine], 1), np.concatenate([-sine, cosine], 1)], 0) * weighting
    for p in range(npy):
        own = y_angle[:, p * y_local:(p + 1) * y_local]
        high, low = split_np(np.concatenate([np.cos(own), np.sin(own)], 0))
        t_forward.append(np.concatenate([high, low], 1))
        high, low = split_np(np.concatenate([np.cos(own), -np.sin(own)], 0).T)
        t_back.append(np.concatenate([high, low], 1))
        order = halves[p]
        rows = z_rows.reshape(2, npy, half, 2 * nz)[:, order].reshape(2 * mz, 2 * nz)
        z_forward.append(np.concatenate(split_np(rows), 0))
        rows = z_inv.reshape(2, npy, half, 2 * nz)[:, order].reshape(2 * mz, 2 * nz)
        high, low = split_np(rows)
        z_back.append(np.concatenate([high, high, low], 0))
    t_forward, t_back, z_forward, z_back = [
        lax.dynamic_index_in_dim(jnp.asarray(np.stack(table)), py, 0, keepdims=False)
        for table in (t_forward, t_back, z_forward, z_back)]

    x_angle = angles(kept(nx, mx), np.arange(nx), nx).T
    cosine, sine = np.cos(x_angle), np.sin(x_angle)
    x_forward = np.zeros((2, nx, 256))
    x_forward[0, :, :mx], x_forward[0, :, 128:128 + mx] = cosine, -sine
    x_forward[1, :, :mx], x_forward[1, :, 128:128 + mx] = sine, cosine
    x_back = np.zeros((2, nx, 256))
    x_back[0, :, :mx], x_back[0, :, 128:128 + mx] = cosine, -sine
    x_back[1, :, :mx], x_back[1, :, 128:128 + mx] = sine, cosine
    x_forward = [jnp.asarray(t.reshape(2 * nx, 256)) for t in split_np(x_forward)]
    x_back = [jnp.asarray(t.reshape(2 * nx, 256)) for t in split_np(x_back)]

    cells = field[0]
    xb = 8 if direct else 1
    per_step = 4 if direct else 1
    grid = (x_local // xb, xb // per_step)
    limit = 60 * 2**20
    params = pltpu.CompilerParams(
        dimension_semantics=("arbitrary", "arbitrary"), vmem_limit_bytes=limit)
    swap = [(0, 1), (1, 0)]

    def field_spec(size, at):
        return pl.BlockSpec(
            (size, per_step, y_local, nz), lambda a, b: (at, a * grid[1] + b, 0, 0))

    def wide_of(count):
        lanes = 2 * count * my
        if direct:
            return (half, lanes // 128, x_local, 128), pl.BlockSpec(
                (half, lanes // 128, xb, 128), lambda a, b: (0, 0, a, 0))
        return (x_local, half, lanes), pl.BlockSpec((1, half, lanes), lambda a, b: (a, 0, 0))

    def to_modes(units):
        count = len(units) * per_unit
        shape, spec = wide_of(count)
        own, other = pl.pallas_call(
            functools.partial(forward_kernel, direct, my, len(units)),
            name="forward_yz",
            out_shape=[jax.ShapeDtypeStruct(shape, F32)] * 2,
            grid=grid,
            in_specs=[field_spec(per_unit, u) for u in units]
            + [whole_spec(t_forward.shape), whole_spec(z_forward.shape)],
            out_specs=[spec, spec],
            scratch_shapes=[pltpu.VMEM((count * my, 2 * nz), BF16)] * (2 * per_step),
            compiler_params=params,
            cost_estimate=pl.CostEstimate(
                flops=count * x_local * 40_000_000, transcendentals=0,
                bytes_accessed=count * x_local * y_local * nz * 4),
        )(*[cells] * len(units), t_forward, z_forward)
        summed = own + lax.ppermute(other, "py", swap)
        if direct:
            return lax.all_to_all(summed, "px", split_axis=0, concat_axis=0, tiled=True)
        send = summed.reshape(x_local, half, 2, count, per_kz, modes).transpose(1, 4, 2, 0, 3, 5)
        got = lax.all_to_all(
            send.reshape(npx, 2, x_local, count * modes), "px", split_axis=0, concat_axis=0,
            tiled=True)
        got = got.reshape(npx, 2, x_local, count, modes).transpose(0, 2, 1, 3, 4)
        got = jnp.pad(got, ((0, 0),) * 4 + ((0, held - modes),)).reshape(nx, 2 * count * held)
        tiles = -(-got.shape[1] // 128)
        got = jnp.pad(got, ((0, 0), (0, tiles * 128 - got.shape[1])))
        return got.reshape(1, nx, tiles, 128).transpose(0, 2, 1, 3)

    def mix(got, units, before, out_units):
        count, outs = len(units) * per_unit, len(out_units) * per_unit
        first = out_units[0] * per_unit
        last = before is not None or len(units) == len(every)
        blocks, _, rows, _ = got.shape

        def weight_spec(u):
            return pl.BlockSpec((2, per_unit, 1, modes, mx), lambda o: (0, u, first + o, 0, 0))

        specs = [whole_spec(got.shape)] + [whole_spec((2 * nx, 256))] * 2
        specs += [weight_spec(u) for u in units]
        operands = [got, *x_forward] + [spectral_weight] * len(units)
        if before is not None:
            specs.append(pl.BlockSpec((1, 2, modes, mx), lambda o: (first + o, 0, 0, 0)))
            operands.append(before)
        scratch = [pltpu.VMEM((count, held, mx), F32)] * 2
        if last:
            specs += [whole_spec((2 * nx, 256))] * 2
            operands += x_back
            shape = (blocks, -(-2 * outs * held // 128), rows, 128)
            out_spec = whole_spec(shape)
            padded = outs * held if direct else shape[1] * 64
            scratch += [pltpu.VMEM((padded, 256), BF16)] * 2
        else:
            shape = (outs, 2, modes, mx)
            out_spec = pl.BlockSpec((1, 2, modes, mx), lambda o: (o, 0, 0, 0))
        return pl.pallas_call(
            functools.partial(mix_kernel, len(units), before is not None, last),
            name="mix_x",
            out_shape=jax.ShapeDtypeStruct(shape, F32),
            grid=(outs,),
            in_specs=specs,
            out_specs=out_spec,
            scratch_shapes=scratch,
            compiler_params=pltpu.CompilerParams(
                dimension_semantics=("arbitrary",), vmem_limit_bytes=limit),
            cost_estimate=pl.CostEstimate(
                flops=count * outs * 40_000_000, transcendentals=0,
                bytes_accessed=4 * count * outs * modes * 128),
        )(*operands)

    def send_back(mixed, count):
        if direct:
            return lax.all_to_all(mixed, "px", split_axis=0, concat_axis=0, tiled=True)
        tiles = mixed.shape[1]
        mixed = mixed.transpose(0, 2, 1, 3).reshape(npx, x_local, tiles * 128)
        mixed = mixed[..., :2 * count * held].reshape(npx, x_local, 2, count, held)[..., :modes]
        back = lax.all_to_all(mixed, "px", split_axis=0, concat_axis=0, tiled=True)
        return back.reshape(half, per_kz, x_local, 2, count, modes).transpose(
            2, 0, 3, 4, 1, 5).reshape(x_local, half, 2 * count * my)

    kron = jnp.kron(pointwise_weight.T.astype(F32), jnp.eye(16, dtype=F32)).astype(BF16)

    def to_cells(back, units, so_far):
        count = len(units) * per_unit
        first = units[0] * per_unit
        partner = lax.ppermute(back, "py", swap)
        _, spec = wide_of(count)
        weights = kron[first * 16:(first + count) * 16]
        operands = [back, partner, cells, z_back, t_back, weights, bias]
        specs = [spec, spec, field_spec(channels, 0), whole_spec(z_back.shape),
                 whole_spec(t_back.shape), whole_spec(weights.shape),
                 pl.BlockSpec(memory_space=pltpu.SMEM)]
        chained = so_far is not None
        if chained:
            operands.append(so_far)
            specs.append(pl.BlockSpec(memory_space=pl.ANY))
        return pl.pallas_call(
            functools.partial(inverse_kernel, direct, my, first, int(chained)),
            name="inverse_zy",
            out_shape=jax.ShapeDtypeStruct(cells.shape, BF16),
            grid=grid,
            in_specs=specs,
            out_specs=field_spec(count, first // count),
            scratch_shapes=([pltpu.VMEM((count * my, 2 * nz), BF16)] * 2
                            + [pltpu.VMEM((count, y_local, nz), F32)]) * per_step,
            input_output_aliases={7: 0} if chained else {},
            compiler_params=params,
            cost_estimate=pl.CostEstimate(
                flops=count * x_local * 60_000_000, transcendentals=0,
                bytes_accessed=count * x_local * y_local * nz * 6),
        )(*operands)

    if direct and len(every) == 5:
        in_chunks, out_chunks = [every[:2], every[2:]], [every[:2], every[2:4], every[4:]]
    else:
        in_chunks, out_chunks = [every], [every]
    before = None
    for units in in_chunks[:-1]:
        before = mix(to_modes(units), units, before, every)
    got = to_modes(in_chunks[-1])
    returned = []
    for units in out_chunks:
        mixed = mix(got, in_chunks[-1], before, units)
        returned.append(send_back(mixed, len(units) * per_unit))
    out = None
    for back, units in zip(returned, out_chunks):
        out = to_cells(back, units, out)
    return out[None]


def solution(mesh):
    def per_part(field, spectral_weight, pointwise_weight, bias):
        rows, mx = spectral_weight.shape[3] * mesh.shape["px"] * mesh.shape["py"], spectral_weight.shape[4]
        mz = field.shape[4] // 4
        return per_device((mx, rows // mz, mz), field, spectral_weight, pointwise_weight, bias)

    in_specs = (
        P("groups", None, "px", "py", None),
        P(None, None, None, ("py", "px"), None),
        P(),
        P(),
    )
    out_specs = P("groups", None, "px", "py", None)
    return jax.shard_map(
        per_part, mesh=mesh, in_specs=in_specs, out_specs=out_specs, check_vma=False
    )
```

```python
import functools

import jax
import jax.numpy as jnp
import numpy as np
from jax import lax
from jax.experimental import pallas as pl
from jax.experimental.pallas import tpu as pltpu
from jax.sharding import PartitionSpec as P


BF16 = jnp.bfloat16
F32 = jnp.float32


def kept(length, retained):
    index = np.arange(retained)
    return np.where(index < retained // 2, index, length - retained + index)


def angles(frequency, positions, length):
    return 2 * np.pi * (np.outer(frequency, positions) % length) / length


def split_np(table):
    high = table.astype(np.float32).astype(BF16)
    low = (table - high.astype(np.float64)).astype(np.float32).astype(BF16)
    return high, low


def split(values):
    high = values.astype(BF16)
    return high, (values - high.astype(F32)).astype(BF16)


def dot(a, b):
    return jnp.dot(a, b, preferred_element_type=F32)


def dot_nt(a, b):
    return lax.dot_general(a, b, (((1,), (1,)), ((), ())), preferred_element_type=F32)


def dot_tn(a, b):
    return lax.dot_general(a, b, (((0,), (0,)), ((), ())), preferred_element_type=F32)


def forward_kernel(direct, my, units, *refs):
    fields, (t_ref, z_ref, own_ref, other_ref), scratch = (
        refs[:units], refs[units:units + 4], refs[units + 4:])
    per_unit, count, _, nz = fields[0].shape
    py = lax.axis_index("py")
    table = t_ref[py]
    z_ref = z_ref.at[py]
    for k in range(count):
        g_high, g_low = scratch[2 * k:2 * k + 2]
        for c in range(units * per_unit):
            cells = fields[c // per_unit][c % per_unit, k]
            high, low = split(dot(table, jnp.concatenate([cells, cells], 0)))
            rows = slice(c * my, (c + 1) * my)
            for q in range(2):
                g_high[rows, q * nz:(q + 1) * nz] = high[q * my:(q + 1) * my]
                g_low[rows, q * nz:(q + 1) * nz] = low[q * my:(q + 1) * my]
    modes = z_ref.shape[0] // 2
    half = modes // 4
    for k in range(count):
        g_high, g_low = scratch[2 * k:2 * k + 2]
        first = dot_nt(z_ref[...], g_high[...])
        out = first[:modes] + first[modes:] + dot_nt(z_ref[:modes], g_low[...])
        out = jnp.concatenate([out[:modes // 2], out[modes // 2:]], 1)
        for ref, part in ((own_ref, out[:half]), (other_ref, out[half:])):
            if direct:
                tiles, xb = ref.shape[1:3]
                flat = ref.reshape(half * tiles * xb, 128)
                at = pl.program_id(1) * count + k
                for t in range(tiles):
                    flat[pl.ds(t * xb + at, half, stride=tiles * xb), :] = part[
                        :, t * 128:(t + 1) * 128]
            else:
                ref[0] = part


def mix_kernel(units, has_before, last, *refs):
    got_ref, forward_high, forward_low = refs[:3]
    weights, refs = refs[3:3 + units], refs[3 + units:]
    if has_before:
        before_ref, refs = refs[0], refs[1:]
    if last:
        back_high, back_low, out_ref, s_real, s_imag, m_high, m_low = refs
    else:
        out_ref, s_real, s_imag = refs
    o = pl.program_id(0)
    blocks, tiles, rows, _ = got_ref.shape
    channels, held, mx = s_real.shape
    per_unit = channels // units
    modes = weights[0].shape[3]
    lanes = channels * held

    @pl.when(o == 0)
    def _():
        got = jnp.concatenate(
            [got_ref[:, t].reshape(blocks * rows, 128) for t in range(tiles)], 1)
        high, low = split(jnp.concatenate([got[:, :lanes], got[:, lanes:2 * lanes]], 0))
        spectrum = dot_tn(high, forward_high[...]) + (
            dot_tn(low, forward_high[...]) + dot_tn(high, forward_low[...]))
        for i in range(channels):
            s_real[i] = spectrum[i * held:(i + 1) * held, :mx]
            s_imag[i] = spectrum[i * held:(i + 1) * held, 128:128 + mx]
        if last:
            m_high[...] = jnp.zeros_like(m_high)
            m_low[...] = jnp.zeros_like(m_low)

    if has_before:
        real, imag = before_ref[0, 0], before_ref[0, 1]
    else:
        real, imag = jnp.zeros((modes, mx), F32), jnp.zeros((modes, mx), F32)
    for i in range(channels):
        w_real = weights[i // per_unit][0, i % per_unit, 0].astype(F32)
        w_imag = weights[i // per_unit][1, i % per_unit, 0].astype(F32)
        in_real = s_real[i, :modes]
        in_imag = s_imag[i, :modes]
        real += w_real * in_real - w_imag * in_imag
        imag += w_real * in_imag + w_imag * in_real
    if not last:
        out_ref[0, 0] = real
        out_ref[0, 1] = imag
        return
    at_row = pl.ds(pl.multiple_of(o * held, held), modes)
    for at, values in ((0, real), (128, imag)):
        high, low = split(values)
        m_high[at_row, at:at + mx] = high
        m_low[at_row, at:at + mx] = low

    @pl.when(o == pl.num_programs(0) - 1)
    def _():
        high = m_high[...]
        low = m_low[...]
        back = dot_nt(back_high[...], high) + (
            dot_nt(back_high[...], low) + dot_nt(back_low[...], high))
        back = jnp.concatenate([back[:blocks * rows], back[blocks * rows:]], 1)
        for t in range(out_ref.shape[1]):
            out_ref[:, t] = back[:, t * 128:(t + 1) * 128].reshape(blocks, rows, 128)


def inverse_kernel(direct, my, start, chained, *refs):
    (own_ref, other_ref, field_ref, z_ref, t_ref, pw_ref, bias_ref) = refs[:7]
    out_ref, scratch = refs[7 + chained], refs[8 + chained:]
    py = lax.axis_index("py")
    t_ref, z_ref = t_ref.at[py], z_ref.at[py]
    channels, count, ny, nz = field_ref.shape
    outs = out_ref.shape[0]
    lanes = outs * my
    group = 16
    for k in range(count):
        v_high, v_low, local = scratch[3 * k:3 * k + 3]
        parts = []
        for ref in (own_ref, other_ref):
            if direct:
                half, tiles, xb, _ = ref.shape
                flat = ref.reshape(half * tiles * xb, 128)
                at = pl.program_id(1) * count + k
                parts.append(jnp.concatenate(
                    [flat[pl.ds(t * xb + at, half, stride=tiles * xb), :] for t in range(tiles)], 1))
            else:
                parts.append(ref[0])
        wide = jnp.concatenate(parts, 0)
        high, low = split(jnp.concatenate([wide[:, :lanes], wide[:, lanes:2 * lanes]], 0))
        high, low = split(dot_tn(jnp.concatenate([high, low, high], 0), z_ref[...]))
        v_high[...] = high
        v_low[...] = low
        for g in range(0, ny, 2 * group):
            pair = [field_ref[:, k, g + j * group:g + (j + 1) * group, :].reshape(
                channels * group, nz) for j in range(2)]
            both = dot(pw_ref[...], jnp.concatenate(pair, 1))
            for j in range(2):
                local[:, g + j * group:g + (j + 1) * group, :] = both[
                    :, j * nz:(j + 1) * nz].reshape(outs, group, nz)
    taps = 2 * my
    for k in range(count):
        v_high, v_low, local = scratch[3 * k:3 * k + 3]
        for c in range(outs):
            rows = slice(c * my, (c + 1) * my)
            top = [v_high[rows, q * nz:(q + 1) * nz] for q in range(2)]
            rest = [v_low[rows, q * nz:(q + 1) * nz] for q in range(2)]
            total = dot(t_ref[:, :2 * taps], jnp.concatenate(top + top, 0)) + dot(
                t_ref[:, :taps], jnp.concatenate(rest, 0))
            total = total + local[c] + bias_ref[start + c]
            out_ref[c, k] = jax.nn.gelu(total).astype(BF16)


def whole_spec(shape):
    return pl.BlockSpec(shape, lambda *_: (0,) * len(shape))


def per_device(sizes, field, spectral_weight, pointwise_weight, bias):
    mx, my, mz = sizes
    samples, channels, x_local, y_local, nz = field.shape
    npx, npy = lax.axis_size("px"), lax.axis_size("py")
    assert samples == 1 and npy == 2
    nx, ny = x_local * npx, y_local * npy
    modes = spectral_weight.shape[3]
    per_kz = my // modes
    held = -(-modes // 16) * 16
    half = mz // npy
    per_unit = 4 if channels % 4 == 0 else channels
    direct = x_local % 8 == 0 and per_kz == 1 and 2 * per_unit * my % 128 == 0
    every = list(range(channels // per_unit))
    halves = np.array([[0, 1], [1, 0]])

    y_angle = angles(kept(ny, my), np.arange(ny), ny)
    t_forward, t_back, z_forward, z_back = [], [], [], []
    z_angle = angles(np.arange(mz), np.arange(nz), nz)
    cosine, sine = np.cos(z_angle), np.sin(z_angle)
    weighting = (np.where(np.arange(mz) == 0, 1.0, 2.0) / (nx * ny * nz))[:, None]
    z_rows = np.stack([np.concatenate([cosine, -sine], 1), np.concatenate([-sine, -cosine], 1)], 0)
    z_inv = np.stack([np.concatenate([cosine, sine], 1), np.concatenate([-sine, cosine], 1)], 0) * weighting
    for p in range(npy):
        own = y_angle[:, p * y_local:(p + 1) * y_local]
        high, low = split_np(np.concatenate([np.cos(own), np.sin(own)], 0))
        t_forward.append(np.concatenate([high, low], 1))
        high, low = split_np(np.concatenate([np.cos(own), -np.sin(own)], 0).T)
        t_back.append(np.concatenate([high, low], 1))
        order = halves[p]
        rows = z_rows.reshape(2, npy, half, 2 * nz)[:, order].reshape(2 * mz, 2 * nz)
        z_forward.append(np.concatenate(split_np(rows), 0))
        rows = z_inv.reshape(2, npy, half, 2 * nz)[:, order].reshape(2 * mz, 2 * nz)
        high, low = split_np(rows)
        z_back.append(np.concatenate([high, high, low], 0))
    t_forward, t_back, z_forward, z_back = [
        jnp.asarray(np.stack(table))
        for table in (t_forward, t_back, z_forward, z_back)]

    x_angle = angles(kept(nx, mx), np.arange(nx), nx).T
    cosine, sine = np.cos(x_angle), np.sin(x_angle)
    x_forward = np.zeros((2, nx, 256))
    x_forward[0, :, :mx], x_forward[0, :, 128:128 + mx] = cosine, -sine
    x_forward[1, :, :mx], x_forward[1, :, 128:128 + mx] = sine, cosine
    x_back = np.zeros((2, nx, 256))
    x_back[0, :, :mx], x_back[0, :, 128:128 + mx] = cosine, -sine
    x_back[1, :, :mx], x_back[1, :, 128:128 + mx] = sine, cosine
    x_forward = [jnp.asarray(t.reshape(2 * nx, 256)) for t in split_np(x_forward)]
    x_back = [jnp.asarray(t.reshape(2 * nx, 256)) for t in split_np(x_back)]

    cells = field[0]
    xb = 8 if direct else 1
    per_step = 4 if direct else 1
    grid = (x_local // xb, xb // per_step)
    limit = 60 * 2**20
    params = pltpu.CompilerParams(
        dimension_semantics=("arbitrary", "arbitrary"), vmem_limit_bytes=limit)
    swap = [(0, 1), (1, 0)]

    def field_spec(size, at):
        return pl.BlockSpec(
            (size, per_step, y_local, nz), lambda a, b: (at, a * grid[1] + b, 0, 0))

    def wide_of(count):
        lanes = 2 * count * my
        if direct:
            return (half, lanes // 128, x_local, 128), pl.BlockSpec(
                (half, lanes // 128, xb, 128), lambda a, b: (0, 0, a, 0))
        return (x_local, half, lanes), pl.BlockSpec((1, half, lanes), lambda a, b: (a, 0, 0))

    def to_modes(units):
        count = len(units) * per_unit
        shape, spec = wide_of(count)
        own, other = pl.pallas_call(
            functools.partial(forward_kernel, direct, my, len(units)),
            name="forward_yz",
            out_shape=[jax.ShapeDtypeStruct(shape, F32)] * 2,
            grid=grid,
            in_specs=[field_spec(per_unit, u) for u in units]
            + [whole_spec(t_forward.shape), whole_spec(z_forward.shape)],
            out_specs=[spec, spec],
            scratch_shapes=[pltpu.VMEM((count * my, 2 * nz), BF16)] * (2 * per_step),
            compiler_params=params,
            cost_estimate=pl.CostEstimate(
                flops=count * x_local * 40_000_000, transcendentals=0,
                bytes_accessed=count * x_local * y_local * nz * 4),
        )(*[cells] * len(units), t_forward, z_forward)
        summed = own + lax.ppermute(other, "py", swap)
        if direct:
            return lax.all_to_all(summed, "px", split_axis=0, concat_axis=0, tiled=True)
        send = summed.reshape(x_local, half, 2, count, per_kz, modes).transpose(1, 4, 2, 0, 3, 5)
        got = lax.all_to_all(
            send.reshape(npx, 2, x_local, count * modes), "px", split_axis=0, concat_axis=0,
            tiled=True)
        got = got.reshape(npx, 2, x_local, count, modes).transpose(0, 2, 1, 3, 4)
        got = jnp.pad(got, ((0, 0),) * 4 + ((0, held - modes),)).reshape(nx, 2 * count * held)
        tiles = -(-got.shape[1] // 128)
        got = jnp.pad(got, ((0, 0), (0, tiles * 128 - got.shape[1])))
        return got.reshape(1, nx, tiles, 128).transpose(0, 2, 1, 3)

    def mix(got, units, before, out_units):
        count, outs = len(units) * per_unit, len(out_units) * per_unit
        first = out_units[0] * per_unit
        last = before is not None or len(units) == len(every)
        blocks, _, rows, _ = got.shape

        def weight_spec(u):
            return pl.BlockSpec((2, per_unit, 1, modes, mx), lambda o: (0, u, first + o, 0, 0))

        specs = [whole_spec(got.shape)] + [whole_spec((2 * nx, 256))] * 2
        specs += [weight_spec(u) for u in units]
        operands = [got, *x_forward] + [spectral_weight] * len(units)
        if before is not None:
            specs.append(pl.BlockSpec((1, 2, modes, mx), lambda o: (first + o, 0, 0, 0)))
            operands.append(before)
        scratch = [pltpu.VMEM((count, held, mx), F32)] * 2
        if last:
            specs += [whole_spec((2 * nx, 256))] * 2
            operands += x_back
            shape = (blocks, -(-2 * outs * held // 128), rows, 128)
            out_spec = whole_spec(shape)
            padded = outs * held if direct else shape[1] * 64
            scratch += [pltpu.VMEM((padded, 256), BF16)] * 2
        else:
            shape = (outs, 2, modes, mx)
            out_spec = pl.BlockSpec((1, 2, modes, mx), lambda o: (o, 0, 0, 0))
        return pl.pallas_call(
            functools.partial(mix_kernel, len(units), before is not None, last),
            name="mix_x",
            out_shape=jax.ShapeDtypeStruct(shape, F32),
            grid=(outs,),
            in_specs=specs,
            out_specs=out_spec,
            scratch_shapes=scratch,
            compiler_params=pltpu.CompilerParams(
                dimension_semantics=("arbitrary",), vmem_limit_bytes=limit),
            cost_estimate=pl.CostEstimate(
                flops=count * outs * 40_000_000, transcendentals=0,
                bytes_accessed=4 * count * outs * modes * 128),
        )(*operands)

    def send_back(mixed, count):
        if direct:
            return lax.all_to_all(mixed, "px", split_axis=0, concat_axis=0, tiled=True)
        tiles = mixed.shape[1]
        mixed = mixed.transpose(0, 2, 1, 3).reshape(npx, x_local, tiles * 128)
        mixed = mixed[..., :2 * count * held].reshape(npx, x_local, 2, count, held)[..., :modes]
        back = lax.all_to_all(mixed, "px", split_axis=0, concat_axis=0, tiled=True)
        return back.reshape(half, per_kz, x_local, 2, count, modes).transpose(
            2, 0, 3, 4, 1, 5).reshape(x_local, half, 2 * count * my)

    kron = jnp.kron(pointwise_weight.T.astype(F32), jnp.eye(16, dtype=F32)).astype(BF16)

    def to_cells(back, units, so_far):
        count = len(units) * per_unit
        first = units[0] * per_unit
        partner = lax.ppermute(back, "py", swap)
        _, spec = wide_of(count)
        operands = [back, partner, cells, z_back, t_back, kron, bias]
        specs = [spec, spec, field_spec(channels, 0), whole_spec(z_back.shape),
                 whole_spec(t_back.shape),
                 pl.BlockSpec((count * 16, channels * 16), lambda a, b: (first // count, 0)),
                 pl.BlockSpec(memory_space=pltpu.SMEM)]
        chained = so_far is not None
        if chained:
            operands.append(so_far)
            specs.append(pl.BlockSpec(memory_space=pl.ANY))
        return pl.pallas_call(
            functools.partial(inverse_kernel, direct, my, first, int(chained)),
            name="inverse_zy",
            out_shape=jax.ShapeDtypeStruct(cells.shape, BF16),
            grid=grid,
            in_specs=specs,
            out_specs=field_spec(count, first // count),
            scratch_shapes=([pltpu.VMEM((count * my, 2 * nz), BF16)] * 2
                            + [pltpu.VMEM((count, y_local, nz), F32)]) * per_step,
            input_output_aliases={7: 0} if chained else {},
            compiler_params=params,
            cost_estimate=pl.CostEstimate(
                flops=count * x_local * 60_000_000, transcendentals=0,
                bytes_accessed=count * x_local * y_local * nz * 6),
        )(*operands)

    if direct and len(every) == 5:
        in_chunks, out_chunks = [every[:2], every[2:]], [every[:2], every[2:4], every[4:]]
    else:
        in_chunks, out_chunks = [every], [every]
    before = None
    for units in in_chunks[:-1]:
        before = mix(to_modes(units), units, before, every)
    got = to_modes(in_chunks[-1])
    returned = []
    for units in out_chunks:
        mixed = mix(got, in_chunks[-1], before, units)
        returned.append(send_back(mixed, len(units) * per_unit))
    out = None
    for back, units in zip(returned, out_chunks):
        out = to_cells(back, units, out)
    return out[None]


def solution(mesh):
    def per_part(field, spectral_weight, pointwise_weight, bias):
        rows, mx = spectral_weight.shape[3] * mesh.shape["px"] * mesh.shape["py"], spectral_weight.shape[4]
        mz = field.shape[4] // 4
        return per_device((mx, rows // mz, mz), field, spectral_weight, pointwise_weight, bias)

    in_specs = (
        P("groups", None, "px", "py", None),
        P(None, None, None, ("py", "px"), None),
        P(),
        P(),
    )
    out_specs = P("groups", None, "px", "py", None)
    return jax.shard_map(
        per_part, mesh=mesh, in_specs=in_specs, out_specs=out_specs, check_vma=False
    )
```
